32 devices in a mesh: seq: 8 (over y, x, core), chan: 4 (over z).
Axes of the slice: x: 2, y: 2, z: 4, core: 2. Of those that a mesh axis runs over, the one named last changes fastest.
Arguments:
- hidden: float32 [8192, 768], P('seq'), may hold values from -6 to 6
- norm1_gain: float32 [768], replicated, may hold values from 0.5 to 1.5
- in_weight: float32 [2, 768, 1536], P(None, None, 'chan'), may hold values from -0.21875 to 0.21875
- conv_weight: float32 [4, 1536], P(None, 'chan'), may hold values from -3 to 3
- conv_bias: float32 [1536], P('chan'), may hold values from -3 to 3
- xproj_weight: float32 [1536, 80], P('chan'), may hold values from -0.078125 to 0.078125
- dtproj_weight: float32 [48, 1536], P(None, 'chan'), may hold values from -0.875 to 0.875
- dt_bias: float32 [1536], P('chan'), may hold values from -1.5 to 0.5
- a_log: float32 [16, 1536], P(None, 'chan'), may hold values from -12 to -1.2
- skip_weight: float32 [1536], P('chan'), may hold values from -4 to 4
- out_weight: float32 [1536, 768], P('chan'), may hold values from -0.15625 to 0.15625
- norm2_gain: float32 [768], replicated, may hold values from 0.5 to 1.5
- router_weight: float32 [768, 8], replicated, may hold values from -0.21875 to 0.21875
- up_weight: float32 [8, 768, 3072], P('seq', None, 'chan'), may hold values from -0.21875 to 0.21875
- down_weight: float32 [8, 3072, 768], P('seq', 'chan'), may hold values from -0.875 to 0.875
- seq_lengths: int32 [3], replicated, may hold values from 1 to 7168, as said below
- expert_ids: int32 [8192, 1], P('seq'), may hold values from 0 to 7; in each aligned block of 1024 rows (0 to 1023, 1024 to 2047, ...) at most 160 rows name the same one
- cotangent: float32 [8192, 768], P('seq'), may hold values from -6 to 6
Outputs:
- output: float32 [8192, 768], P('seq')
- hidden_grad: float32 [8192, 768], P('seq')
- norm1_gain_grad: float32 [768], replicated
- in_weight_grad: float32 [2, 768, 1536], P(None, None, 'chan')
- conv_weight_grad: float32 [4, 1536], P(None, 'chan')
- conv_bias_grad: float32 [1536], P('chan')
- xproj_weight_grad: float32 [1536, 80], P('chan')
- dtproj_weight_grad: float32 [48, 1536], P(None, 'chan')
- dt_bias_grad: float32 [1536], P('chan')
- a_log_grad: float32 [16, 1536], P(None, 'chan')
- skip_weight_grad: float32 [1536], P('chan')
- out_weight_grad: float32 [1536, 768], P('chan')
- norm2_gain_grad: float32 [768], replicated
- router_weight_grad: float32 [768, 8], replicated
- up_weight_grad: float32 [8, 768, 3072], P('seq', None, 'chan')
- down_weight_grad: float32 [8, 3072, 768], P('seq', 'chan')
The draws below stay inside these ranges and needn't reach their ends.
Inputs may be any that keep to these rules, and one draw needn't show every extreme that they name: `seq_lengths`: the 3 lengths sum to 8192; the middle one is exactly 7168, and the first and last sum to 1024, each at least 1. `expert_ids`: among the 1024 tokens of one index of seq no expert is named more than 160 times, and in every draw some expert is named exactly 160 times by the tokens of some index.
All inputs are finite; a program needn't handle non-finite values.
Results may differ from the reference program's by a relative error of at most 0.0003.
Values sent between devices are 32-bit elements; how exact they have to be, the bound alone decides.
No kernel may reach another device: no remote copies, remote signals or barrier semaphores. Data moves between devices by JAX's collectives and lax.ppermute only.
A program may use at most 640 MiB of HBM per device.

```python
import math
import jax
import jax.numpy as jnp
import numpy as np
from jax import lax

D = 768
DI = 1536
STATE = 16
DT_RANK = 48
KERNEL = 4
FF = 3072
TOK_DEV = 1024
EXPERTS = 8
CAP = 160
TOKENS = 8192
N_SEQ = 8


def draw_seq_lengths(key, part):
    head_len = jax.random.randint(key, (), 1, TOK_DEV, dtype=jnp.int32)
    middle_len = jnp.full((), TOKENS - TOK_DEV, jnp.int32)
    return jnp.stack([head_len, middle_len, TOK_DEV - head_len]).astype(jnp.int32)


def level_of(stream_key, extent, shards, low, high):
    loudness = 1.0
    for position, parts in shards:
        draws = jax.random.uniform(jax.random.fold_in(jax.random.fold_in(stream_key, 6), position), (parts,), jnp.float32, low / len(shards), high / len(shards))
        loudness = loudness * jnp.repeat(jnp.exp(draws), extent[position] // parts).reshape((-1,) + (1,) * (len(extent) - 1 - position))
    return loudness


def assign_block(rng, own, number, rows, amount, top, bound, skew):
    sequence = jax.random.permutation(rng, amount)
    heavy_load, usual = load_shares(amount, rows * top, bound, skew, True), load_shares(amount, rows * top, bound, skew, False)
    places = jnp.arange(amount)

    def named(lengths, turn):
        used = int((lengths > 0).sum())
        fixed = max(1, used // 4)
        shifted = fixed + (places - fixed + turn * (used - fixed)) % max(1, amount - fixed)
        return jnp.zeros((amount,), jnp.int32).at[sequence[jnp.where(places < fixed, places, shifted)]].set(jnp.asarray(lengths, jnp.int32))

    lengths = jnp.where(number % 4 == 0, named(heavy_load, number // 4), named(usual, number - number // 4 - 1))
    mixed = jax.random.permutation(jax.random.fold_in(own, 3), amount)
    donor, taker = mixed[0:amount // 2 * 2:2], mixed[1:amount // 2 * 2:2]
    room = jnp.minimum(lengths[donor] - 1, bound - lengths[taker]) // 2
    room = jnp.where((donor == sequence[0]) | (taker == sequence[0]) | (lengths[taker] == 0), 0, jnp.maximum(room, 0))
    shifted = jax.random.randint(jax.random.fold_in(own, 4), (amount // 2,), 0, 1 << 20) % (room + 1)
    lengths = lengths.at[donor].add(-shifted).at[taker].add(shifted)
    labels = jnp.searchsorted(jnp.cumsum(lengths), jnp.arange(rows * top), side="right").astype(jnp.int32)
    listing = labels.reshape(top, rows).T
    listing = listing[jax.random.permutation(jax.random.fold_in(own, 1), rows)]
    turn = jax.random.randint(jax.random.fold_in(own, 2), (rows, 1), 0, top)
    return jnp.take_along_axis(listing, (jnp.arange(top)[None, :] + turn) % top, axis=1)


def load_shares(number_of, total, bound, skew, full):
    portions = [(1 << 20) // math.isqrt(rank ** skew) + 1 for rank in range(1, number_of + 1)]
    largest = bound if full else min(bound, max(-(-total // number_of), total * portions[0] // sum(portions)))
    least = 1 if total - largest >= number_of - 1 else 0
    given, surplus = [largest] + [least] * (number_of - 1), total - largest - least * (number_of - 1)
    while surplus > 0:
        candidates = [i for i in range(1, number_of) if given[i] < largest] or [i for i in range(1, number_of) if given[i] < bound]
        mass, budget = sum([portions[i] for i in candidates]), surplus
        for i in candidates:
            addition = min(bound - given[i], max(1, budget * portions[i] // mass), surplus)
            given[i] = given[i] + addition
            surplus = surplus - addition
    return np.array(given)


def centred(rng, shape, deviation, bound, cuts=(), held_as=jnp.bfloat16):
    array = jax.random.normal(rng, shape, jnp.float32) * deviation
    if len(cuts) > 0:
        array = level_of(rng, shape, cuts, -0.22, 0.18) * array
    return jnp.clip(array, min=-bound, max=bound).astype(held_as)


def setup_inputs(seed: int = 0) -> dict:
    splits = jax.random.split(jax.random.key(seed), 19)
    hidden = centred(splits[0], (TOKENS, D), 1.0, 6.0, ((0, 8),), jnp.float32)
    norm1_gain = jnp.clip(1.0 + 0.1 * jax.random.normal(splits[1], (D,), jnp.float32), 0.5, 1.5)
    in_weight = centred(splits[2], (2, D, DI), D ** -0.5, 0.21875, ((2, 4),), jnp.float32)
    conv_weight = centred(splits[3], (KERNEL, DI), KERNEL ** -0.5, 3.0, ((1, 4),), jnp.float32)
    conv_bias = centred(splits[4], (DI,), 0.5, 3.0, ((0, 4),), jnp.float32)
    xproj_weight = centred(splits[5], (DI, DT_RANK + 2 * STATE), (DI * 4) ** -0.5, 0.078125, ((0, 4),), jnp.float32)
    dtproj_weight = centred(splits[6], (DT_RANK, DI), DT_RANK ** -0.5, 0.875, ((1, 4),), jnp.float32)
    dt_bias = jnp.clip(-1.5 + 2.0 * jax.random.uniform(splits[7], (DI,), jnp.float32) ** level_of(splits[7], (DI,), ((0, 4),), -0.2, 0.2), -1.5, 0.5)
    a_log = jnp.clip(-12.0 + 10.8 * jax.random.uniform(splits[8], (STATE, DI), jnp.float32) ** level_of(splits[8], (STATE, DI), ((1, 4),), -0.2, 0.2), -12.0, -1.2)
    skip_weight = centred(splits[9], (DI,), 1.0, 4.0, ((0, 4),), jnp.float32)
    out_weight = centred(splits[10], (DI, D), DI ** -0.5, 0.15625, ((0, 4),), jnp.float32)
    norm2_gain = jnp.clip(1.0 + 0.1 * jax.random.normal(splits[11], (D,), jnp.float32), 0.5, 1.5)
    router_weight = centred(splits[12], (D, EXPERTS), D ** -0.5, 0.21875, (), jnp.float32)
    up_weight = centred(splits[13], (EXPERTS, D, FF), D ** -0.5, 0.21875, ((0, 8), (2, 4)), jnp.float32)
    down_weight = centred(splits[14], (EXPERTS, FF, D), (max(1, FF // (EXPERTS * EXPERTS))) ** -0.5, 0.875, ((0, 8), (1, 4)), jnp.float32)
    seq_lengths = draw_seq_lengths(jax.random.fold_in(splits[18], 71), 0)
    expert_ids_keys = jax.random.split(jax.random.fold_in(splits[16], 1), TOKENS // TOK_DEV)
    expert_ids_turns = jax.random.permutation(jax.random.fold_in(splits[16], 3), TOKENS // TOK_DEV)
    expert_ids = jax.vmap(lambda own, number: assign_block(jax.random.fold_in(splits[16], 2), own, number, TOK_DEV, EXPERTS, 1, CAP, 2))(expert_ids_keys, expert_ids_turns).reshape((TOKENS, 1))
    cotangent = centred(splits[17], (TOKENS, D), 1.0, 6.0, ((0, 8),), jnp.float32)
    return dict(hidden=hidden, norm1_gain=norm1_gain, in_weight=in_weight, conv_weight=conv_weight, conv_bias=conv_bias, xproj_weight=xproj_weight, dtproj_weight=dtproj_weight, dt_bias=dt_bias, a_log=a_log, skip_weight=skip_weight, out_weight=out_weight, norm2_gain=norm2_gain, router_weight=router_weight, up_weight=up_weight, down_weight=down_weight, seq_lengths=seq_lengths, expert_ids=expert_ids, cotangent=cotangent)


epsilon = 1e-05

@jax.custom_vjp
def low(v):
    return lax.optimization_barrier(v.astype(jnp.bfloat16)).astype(jnp.float32)

@jax.custom_vjp
def low_back(v):
    return v

def low_keep(v):
    return (low(v), None)

def low_pass(kept, grad):
    return (grad,)

def back_keep(v):
    return (v, None)

def back_low(kept, grad):
    return (low(grad),)
low.defvjp(low_keep, low_pass)
low_back.defvjp(back_keep, back_low)

def matmul(left_side, right_side):
    return jnp.dot(left_side, right_side, precision=lax.Precision.HIGHEST, preferred_element_type=jnp.float32)

def rms_norm(values, gain_vec):
    return values * lax.rsqrt(lax.optimization_barrier(jnp.mean(values * values, axis=-1, keepdims=True)) + epsilon) * gain_vec

def reference(hidden, norm1_gain, in_weight, conv_weight, conv_bias, xproj_weight, dtproj_weight, dt_bias, a_log, skip_weight, out_weight, norm2_gain, router_weight, up_weight, down_weight, seq_lengths, expert_ids, cotangent):
    places = jnp.arange(TOKENS, dtype=jnp.int32)
    seq_ends = jnp.cumsum(seq_lengths, dtype=jnp.int32)
    starts = seq_ends - seq_lengths
    inside = (places[:, None] >= starts[None, :]) & (places[:, None] < seq_ends[None, :])
    seq_start = lax.optimization_barrier(jnp.sum(jnp.where(inside, starts[None, :], 0), axis=1)).astype(jnp.int32)
    offset = places - seq_start
    keeping = (offset > 0).astype(jnp.float32)
    tap_valid = [(offset >= KERNEL - 1 - tap_index).astype(jnp.float32)[:, None] for tap_index in range(KERNEL)]
    chosen = expert_ids[:, 0].astype(jnp.int32)
    one_hot_int = (chosen[:, None] == jnp.arange(EXPERTS, dtype=jnp.int32)[None, :]).astype(jnp.int32)
    one_hot = one_hot_int.astype(jnp.float32)
    token_order = jnp.argsort(chosen, stable=True).astype(jnp.int32)
    counts = lax.optimization_barrier(jnp.sum(one_hot_int, axis=0)).astype(jnp.int32)
    firsts = (jnp.cumsum(counts, dtype=jnp.int32) - counts).astype(jnp.int32)
    lane_ids = jnp.arange(N_SEQ * CAP, dtype=jnp.int32)
    picked = token_order[jnp.clip(firsts[:, None] + lane_ids[None, :], 0, TOKENS - 1)]
    filled = (lane_ids[None, :] < counts[:, None]).astype(jnp.float32)

    def forward(hidden, norm1_gain, in_weight, conv_weight, conv_bias, xproj_weight, dtproj_weight, dt_bias, a_log, skip_weight, out_weight, norm2_gain, router_weight, up_weight, down_weight):
        normed = rms_norm(hidden, norm1_gain)
        inner = matmul(normed, in_weight[0])
        gate_in = matmul(normed, in_weight[1])
        padded = jnp.concatenate([jnp.zeros((KERNEL - 1, DI), jnp.float32), inner], axis=0)
        summed = conv_bias[None, :] + jnp.zeros((TOKENS, DI), jnp.float32)
        for tap_index in range(KERNEL):
            summed = summed + conv_weight[tap_index][None, :] * padded[tap_index:tap_index + TOKENS] * tap_valid[tap_index]
        activated = jax.nn.silu(summed)
        projected = matmul(activated, xproj_weight)
        low_rank = projected[:, :DT_RANK]
        input_coef = projected[:, DT_RANK:DT_RANK + STATE]
        output_coef = projected[:, DT_RANK + STATE:]
        step_size = jax.nn.softplus(matmul(low_rank, dtproj_weight) + dt_bias[None, :])
        decay_rates = -jnp.exp(a_log)

        def token_step(carried, packed):
            step_tok, in_tok, out_tok, act_tok, keep_tok = packed
            updated = jnp.exp(step_tok[None, :] * decay_rates) * carried * keep_tok + in_tok[:, None] * (step_tok * act_tok)[None, :]
            return (updated, lax.optimization_barrier(jnp.sum(out_tok[:, None] * updated, axis=0)))

        def run_block(carried, block_data):
            return lax.scan(token_step, carried, block_data)
        blocks = TOKENS // 128
        packed = tuple((column.reshape((blocks, 128) + column.shape[1:]) for column in (step_size, input_coef, output_coef, activated, keeping)))
        _, scanned = lax.scan(jax.checkpoint(run_block), jnp.zeros((STATE, DI), jnp.float32), packed)
        scan_out = scanned.reshape(TOKENS, DI)
        gated = (scan_out + skip_weight[None, :] * activated) * jax.nn.silu(gate_in)
        residual = hidden + matmul(gated, out_weight)
        normed2 = rms_norm(residual, norm2_gain)
        probabilities = jax.nn.softmax(matmul(normed2, router_weight), axis=-1)
        gate_prob = lax.optimization_barrier(jnp.sum(probabilities * one_hot, axis=-1))

        def one_expert(packed_expert):
            weights_up, weights_down, rows_idx, mask_rows = packed_expert
            gathered = normed2[rows_idx] * mask_rows[:, None]
            return matmul(jax.nn.gelu(matmul(gathered, weights_up), approximate=True), weights_down) * mask_rows[:, None]
        expert_rows = lax.map(one_expert, (up_weight, down_weight, picked, filled))
        expert_out = jnp.zeros((TOKENS, D), jnp.float32).at[picked.reshape(-1)].add(expert_rows.reshape(-1, D))
        return residual + gate_prob[:, None] * expert_out
    output, pullback = jax.vjp(forward, hidden, norm1_gain, in_weight, conv_weight, conv_bias, xproj_weight, dtproj_weight, dt_bias, a_log, skip_weight, out_weight, norm2_gain, router_weight, up_weight, down_weight)
    gradients = pullback(cotangent)
    return (output, gradients[0], gradients[1], gradients[2], gradients[3], gradients[4], gradients[5], gradients[6], gradients[7], gradients[8], gradients[9], gradients[10], gradients[11], gradients[12], gradients[13], gradients[14])
```

```python
import functools

import jax
import jax.numpy as jnp
from jax import lax
from jax.experimental import pallas as pl
from jax.experimental.pallas import tpu as pltpu
from jax.sharding import PartitionSpec as P

EPS = 1e-05
F32 = jnp.float32
BF = jnp.bfloat16
LOG2E = 1.4426950408889634
LN2 = 0.6931471805599453
GELU = 0.7978845608
CUBE = 0.044715
NEVER = 1e30
CHUNKS = 8
QUARTERS = 4
PAD = 128


def shape(dims, dtype=F32):
    return jax.ShapeDtypeStruct(dims, dtype)


def call(kernel, outs, *args, scratch=(), smem=(), flops=0, vmem=40):
    specs = [
        pl.BlockSpec(memory_space=pltpu.SMEM if place in smem else pltpu.VMEM)
        for place in range(len(args))
    ]
    size = sum(a.size * a.dtype.itemsize for a in args)
    leaves = jax.tree.leaves(outs)
    size += sum(o.size * o.dtype.itemsize for o in leaves)
    return pl.pallas_call(
        kernel,
        out_shape=outs,
        in_specs=specs,
        out_specs=jax.tree.map(lambda _: pl.BlockSpec(memory_space=pltpu.VMEM), outs),
        scratch_shapes=list(scratch),
        compiler_params=pltpu.CompilerParams(vmem_limit_bytes=vmem << 20),
        cost_estimate=pl.CostEstimate(flops=int(flops), bytes_accessed=int(size), transcendentals=0),
    )(*args)


def cut(values):
    high = values.astype(BF)
    return high, (values - high.astype(F32)).astype(BF)


def cut3(values):
    high, rest = values.astype(BF), None
    rest = values - high.astype(F32)
    middle = rest.astype(BF)
    return high, middle, (rest - middle.astype(F32)).astype(BF)


def nn(left, right):
    return lax.dot_general(left, right, (((1,), (0,)), ((), ())), preferred_element_type=F32)


def nt(left, right):
    return lax.dot_general(left, right, (((1,), (1,)), ((), ())), preferred_element_type=F32)


def tn(left, right):
    return lax.dot_general(left, right, (((0,), (0,)), ((), ())), preferred_element_type=F32)


def triple(product, left, right):
    return product(left[0], right[0]) + (product(left[0], right[1]) + product(left[1], right[0]))


def pick(marks, values):
    high, middle, low = cut3(values)
    return nn(marks, high) + (nn(marks, middle) + nn(marks, low))


def sigmoid(values):
    return 1.0 / (1.0 + jnp.exp(-values))


def row_marks(first, count, row_ids):
    places = lax.broadcasted_iota(jnp.int32, (count, row_ids.shape[1]), 0) + first
    return (places == row_ids).astype(F32).astype(BF)


def col_marks(column_ids, first, count):
    places = lax.broadcasted_iota(jnp.int32, (column_ids.shape[0], count), 1) + first
    return (places == column_ids).astype(F32).astype(BF)


def enter_kernel(hid, rim, gain, w, cw, cb, xp, msk, inner_o, gate_o, conv_o, act_o, proj_o, whi, wlo):
    rows, chan = gate_o.shape
    for half in range(2):
        high, low = cut(w[half])
        whi[:, half * chan : (half + 1) * chan] = high
        wlo[:, half * chan : (half + 1) * chan] = low

    def project(values):
        scale = lax.rsqrt(jnp.mean(values * values, axis=1, keepdims=True) + EPS)
        return triple(nn, cut(values * scale * gain[...]), (whi[...], wlo[...]))

    lead = project(rim[...])

    def fill(block, _):
        base = pl.multiple_of(block * 256, 256)
        both = project(hid[pl.ds(base, 256), :])
        inner_o[pl.ds(base + 24, 256), :] = both[:, :chan]
        gate_o[pl.ds(base, 256), :] = both[:, chan:]
        return 0

    lax.fori_loop(0, rows // 256, fill, 0)
    top = lax.broadcasted_iota(jnp.int32, (8, chan), 0) == 0
    for i in range(3):
        before = pltpu.roll(inner_o[rows + 8 * i : rows + 8 * i + 8, :], 1, axis=0)
        inner_o[8 * i : 8 * i + 8, :] = jnp.where(top, lead[5 + i : 6 + i, :chan], before)
    xps = cut(xp[...])

    def convolve(block, _):
        base = pl.multiple_of(block * 128, 128)
        marks = msk[pl.ds(base, 128), :]
        summed = cb[...] + cw[3:4, :] * inner_o[pl.ds(base + 24, 128), :]
        for k in range(3):
            summed = summed + cw[k : k + 1, :] * inner_o[pl.ds(base + 8 * k, 128), :] * marks[:, k : k + 1]
        act = summed * sigmoid(summed)
        conv_o[pl.ds(base, 128), :] = summed
        act_o[pl.ds(base, 128), :] = act
        proj_o[block] = triple(nt, xps, cut(act))
        return 0

    lax.fori_loop(0, rows // 128, convolve, 0)


def prefix(totals, states, later):
    places = lax.broadcasted_iota(jnp.int32, totals.shape, 0)
    for hop in (1, 2, 4):
        turn = CHUNKS - hop if later else hop
        ok = places < CHUNKS - hop if later else places >= hop
        far_t, far_s = pltpu.roll(totals, turn, axis=0), pltpu.roll(states, turn, axis=0)
        states = jnp.where(ok, totals * far_s + states, states)
        totals = jnp.where(ok, totals * far_t, totals)
    turn = CHUNKS - 1 if later else 1
    edge = places == (CHUNKS - 1 if later else 0)
    before_t = jnp.where(edge, 1.0, pltpu.roll(totals, turn, axis=0))
    before_s = jnp.where(edge, 0.0, pltpu.roll(states, turn, axis=0))
    return before_t, before_s, totals, states


def chunk_totals(rates, spans, sums, before_t, before_s, total_o, states_n, later):
    for n in range(states_n):
        here = slice(8 * n, 8 * n + 8)
        bt, bs, tt, ts = prefix(jnp.exp2(spans * rates[here, :]), sums[here, :], later)
        before_t[here, :] = bt
        before_s[here, :] = bs
        row = 0 if later else CHUNKS - 1
        total_o[n : n + 1, :] = ts[row : row + 1]
        total_o[states_n + n : states_n + n + 1, :] = tt[row : row + 1]


def sweep1_kernel(proj, dtw, dtb, alog, act, msk, delta_o, pj_o, rate_o, bt_o, bs_o, tot_o, sums, dcut):
    rows, chan = act.shape
    ranks, states_n = dtw.shape[0], alog.shape[0]
    width = proj.shape[1]
    dtws = cut(dtw[...])
    pj_o[...] = jnp.zeros_like(pj_o)
    for block in range(rows // 128):
        turned = proj[block].T
        here = slice(128 * block, 128 * block + 128)
        pj_o[here, :width] = turned
        raw = triple(nn, cut(turned[:, :ranks]), dtws) + dtb[...]
        small = jnp.exp(-jnp.abs(raw))
        up = 1.0 + small
        tail = jnp.where(up == 1.0, small, jnp.log(up) * (small / jnp.where(up == 1.0, 1.0, up - 1.0)))
        step = jnp.maximum(raw, 0.0) + tail
        delta_o[here, :] = step
        dcut[here, :] = jnp.where(msk[here, 3:4] > 0.0, step, NEVER)
    for n in range(states_n):
        rate_o[8 * n : 8 * n + 8, :] = jnp.broadcast_to(-LOG2E * jnp.exp(alog[n : n + 1, :]), (8, chan))
    sums[...] = jnp.zeros_like(sums)

    def step_fn(i, span):
        here = pl.ds(pl.multiple_of(i * 8, 8), 8)
        cutd = dcut[here, :]
        fed = delta_o[here, :] * act[here, :]
        coefs = pj_o[here, :]
        for n in range(states_n):
            at = slice(8 * n, 8 * n + 8)
            col = ranks + n
            factor = jnp.exp2(cutd * rate_o[at, :])
            sums[at, :] = factor * sums[at, :] + jnp.broadcast_to(coefs[:, col : col + 1], (8, chan)) * fed
        return span + cutd

    spans = lax.fori_loop(0, rows // 8, step_fn, jnp.zeros((8, chan), F32))
    chunk_totals(rate_o, spans, sums, bt_o, bs_o, tot_o, states_n, False)


def entering(me, gathered, count, states_n, later):
    def join(turn, held):
        place = count - 1 - turn if later else turn
        piece = gathered[place]
        longer = piece[states_n:] * held + piece[:states_n]
        return jnp.where((place > me) if later else (place < me), longer, held)

    return lax.fori_loop(0, count, join, jnp.zeros(gathered.shape[1:], F32)[:states_n])


def sweep2_kernel(ranks, me, gath, delta, act, pj, gate, msk, rate, bt, bs, skip, first_o, h_o, pre_o, hi_o, lo_o, held):
    steps = delta.shape[0] // 8
    chan = delta.shape[1]
    states_n = rate.shape[0] // 8

    @pl.when(pl.program_id(0) == 0)
    def _():
        enter = entering(me[0], gath, gath.shape[0], states_n, False)
        for n in range(states_n):
            at = slice(8 * n, 8 * n + 8)
            held[at, :] = bt[at, :] * enter[n : n + 1] + bs[at, :]
        first_o[...] = held[...]

    def step_fn(i, _):
        here = pl.ds(pl.multiple_of(i * 8, 8), 8)
        step, value = delta[here, :], act[here, :]
        cutd = jnp.where(msk[here, 3:4] > 0.0, step, NEVER)
        fed = step * value
        coefs = pj[here, :]
        total = jnp.zeros((8, chan), F32)
        base = i * 8 * states_n
        for n in range(states_n):
            at = slice(8 * n, 8 * n + 8)
            into = jnp.broadcast_to(coefs[:, ranks + n : ranks + n + 1], (8, chan))
            out = jnp.broadcast_to(coefs[:, ranks + states_n + n : ranks + states_n + n + 1], (8, chan))
            now = jnp.exp2(cutd * rate[at, :]) * held[at, :] + into * fed
            held[at, :] = now
            h_o[pl.ds(pl.multiple_of(base + 8 * n, 8), 8), :] = now
            total = total + out * now
        pre = total + skip[...] * value
        pre_o[here, :] = pre
        return 0

    lax.fori_loop(0, steps, step_fn, 0)
    gates = gate[...]
    high, low = cut(pre_o[...] * (gates * sigmoid(gates)))
    hi_o[...] = high
    lo_o[...] = low


def leave_kernel(quarter, prow, hi, lo, wout, mixed_o, ghi_o, glo_o):
    count = mixed_o.shape[0]
    marks = row_marks(quarter * count, count, prow[...])
    high, low = nn(marks, hi[...]).astype(BF), nn(marks, lo[...]).astype(BF)
    ghi_o[...] = high
    glo_o[...] = low
    mixed_o[...] = triple(nn, (high, low), cut(wout[...]))


def deal_kernel(prow, hid, cot, hid_o, cot_o):
    count = 256

    def block_fn(block, _):
        base = pl.multiple_of(block * count, count)
        marks = row_marks(base, count, prow[...])
        hid_o[pl.ds(base, count), :] = pick(marks, hid[...])
        cot_o[pl.ds(base, count), :] = pick(marks, cot[...])
        return 0

    lax.fori_loop(0, hid_o.shape[0] // count, block_fn, 0)


def slots_kernel(cot, srow, cslot_o):
    marks = row_marks(0, cslot_o.shape[0], srow[...])
    cslot_o[...] = pick(marks, cot[...])


def route_kernel(mixed, hid, gain, router_t, onehot, srow, res_o, slot_o, gate_o, soft_o):
    model = hid.shape[1]
    residual = hid[...] + mixed[...]
    res_o[...] = residual
    scale = lax.rsqrt(jnp.mean(residual * residual, axis=1, keepdims=True) + EPS)
    normed = residual * scale * gain[...]
    logits = triple(nt, cut(normed), cut(router_t[...]))
    grown = jnp.exp(logits - jnp.max(logits, axis=1, keepdims=True))
    soft = grown / jnp.sum(grown, axis=1, keepdims=True)
    prob = jnp.sum(soft * onehot[...], axis=1, keepdims=True)
    gate_o[...] = prob
    soft_o[...] = soft
    marks = row_marks(0, slot_o.shape[0], srow[...])
    slot_o[:, :model] = pick(marks, normed)
    slot_o[:, model:] = pick(marks, jnp.broadcast_to(prob, (prob.shape[0], PAD)))


def weights_kernel(up, down, uhi, ulo, dhi, dlo):
    uhi[...], ulo[...] = cut(up[...])
    dhi[...], dlo[...] = cut(down[...])


def expert_kernel(xin, cin, uhi, ulo, dhi, dlo, y_o, dx_o, gt_o, gh_o):
    model = cin.shape[1]
    ups, downs = (uhi[...], ulo[...]), (dhi[...], dlo[...])
    before = triple(nn, cut(xin[:, :model]), ups)
    wave = jnp.tanh(GELU * (before + CUBE * before * before * before))
    hidden_units = 0.5 * before * (1.0 + wave)
    slope = 0.5 * (1.0 + wave) + 0.5 * before * (1.0 - wave * wave) * (
        GELU * (1.0 + 3.0 * CUBE * before * before)
    )
    back = triple(nt, cut(cin[...]), downs)
    turned = back * slope
    dx_o[:, :model] = triple(nt, cut(turned), ups)
    dx_o[:, model:] = jnp.broadcast_to(
        jnp.sum(hidden_units * back, axis=1, keepdims=True), (cin.shape[0], PAD)
    )
    y_o[...] = triple(nn, cut(hidden_units), downs)
    prob = xin[:, model : model + 1]
    gt_o[...] = turned * prob
    gh_o[...] = hidden_units * prob


def expert_grads_kernel(*refs):
    count = (len(refs) - 2) // 4
    dup, ddown = refs[-2:]
    model = dup.shape[0]
    for i in range(count):
        x, c, gt, gh = refs[i], refs[count + i], refs[2 * count + i], refs[3 * count + i]
        one = triple(tn, cut(x[:, :model]), cut(gt[...]))
        two = triple(tn, cut(gh[...]), cut(c[...]))
        dup[...] = one if i == 0 else dup[...] + one
        ddown[...] = two if i == 0 else ddown[...] + two


def home_kernel(dxin, scol, prob, soft, onehot, router_t, part_o, dlog_o):
    model = router_t.shape[1]
    marks = col_marks(scol[...], 0, dxin.shape[0])
    rows = pick(marks, dxin[...])
    dlog = rows[:, model : model + 1] * prob[...] * (onehot[...] - soft[...])
    dlog_o[...] = dlog
    part_o[...] = prob[...] * rows[:, :model] + triple(nn, cut(dlog), cut(router_t[...]))


def home_out_kernel(yin, scol, prob, part_o):
    part_o[...] = prob[...] * pick(col_marks(scol[...], 0, yin.shape[0]), yin[...])


def resid_kernel(dn2, res, cot, gain, wout, dlog, dres_o, dgp_o, dgain_o, drouter_o):
    residual, grad = res[...], dn2[...]
    scale = lax.rsqrt(jnp.mean(residual * residual, axis=1, keepdims=True) + EPS)
    unit = residual * scale
    mine = grad * gain[...]
    dres = cot[...] + scale * mine - unit * (scale * jnp.mean(mine * unit, axis=1, keepdims=True))
    dres_o[...] = dres
    dgain_o[...] = jnp.sum(grad * unit, axis=0, keepdims=True)
    drouter_o[...] = triple(tn, cut(dlog[...]), cut(unit * gain[...]))
    dgp_o[...] = triple(nt, cut(dres), cut(wout[...]))


def back1_kernel(ranks, dg0, dg1, dg2, dg3, pcol, gate, pre, act, delta, msk, pj, rate, dscan_o, dgate_o, dskip_o, bt_o, bs_o, tot_o, sums, dcut):
    rows, chan = gate.shape
    states_n = rate.shape[0] // 8
    parts = [cut3(d[...]) for d in (dg0, dg1, dg2, dg3)]
    count = dg0.shape[0]

    def block_fn(block, total):
        here = pl.ds(pl.multiple_of(block * 256, 256), 256)
        grads = jnp.zeros((256, chan), F32)
        for q, (high, middle, low) in enumerate(parts):
            marks = col_marks(pcol[here, :], q * count, count)
            grads = grads + (nn(marks, high) + (nn(marks, middle) + nn(marks, low)))
        gates = gate[here, :]
        soft = sigmoid(gates)
        scanned = grads * (gates * soft)
        dscan_o[here, :] = scanned
        dgate_o[here, :] = grads * pre[here, :] * (soft * (1.0 + gates * (1.0 - soft)))
        dcut[here, :] = jnp.where(msk[here, 3:4] > 0.0, delta[here, :], NEVER)
        return total + jnp.sum(scanned * act[here, :], axis=0, keepdims=True)

    dskip_o[...] = lax.fori_loop(0, rows // 256, block_fn, jnp.zeros((1, chan), F32))
    sums[...] = jnp.zeros_like(sums)
    steps = rows // 8

    def step_fn(turn, span):
        here = pl.ds(pl.multiple_of((steps - 1 - turn) * 8, 8), 8)
        cutd = dcut[here, :]
        grads = dscan_o[here, :]
        coefs = pj[here, :]
        for n in range(states_n):
            at = slice(8 * n, 8 * n + 8)
            col = ranks + states_n + n
            sums[at, :] = jnp.exp2(cutd * rate[at, :]) * (
                sums[at, :] + jnp.broadcast_to(coefs[:, col : col + 1], (8, chan)) * grads
            )
        return span + cutd

    spans = lax.fori_loop(0, steps, step_fn, jnp.zeros((8, chan), F32))
    chunk_totals(rate, spans, sums, bt_o, bs_o, tot_o, states_n, True)


def back2_kernel(ranks, me, gath, first, delta, act, pj, proj, dscan, msk, h, edge, rate, bt, bs, dtw, dact_o, dproj_o, dtw_o, dtb_o, dalog_o, held, rsum, draw, dbc):
    steps = delta.shape[0] // 8
    chan = delta.shape[1]
    states_n = rate.shape[0] // 8
    turn = pl.program_id(0)
    last = turn == pl.num_programs(0) - 1

    @pl.when(turn == 0)
    def _():
        enter = entering(me[0], gath, gath.shape[0], states_n, True)
        for n in range(states_n):
            at = slice(8 * n, 8 * n + 8)
            held[at, :] = bt[at, :] * enter[n : n + 1] + bs[at, :]
        rsum[...] = jnp.zeros_like(rsum)
        dtw_o[...] = jnp.zeros_like(dtw_o)
        dtb_o[...] = jnp.zeros_like(dtb_o)

    lanes = lax.broadcasted_iota(jnp.int32, (8, PAD), 1)

    def one_step(i, before):
        here = pl.ds(pl.multiple_of(i * 8, 8), 8)
        step, value, grads = delta[here, :], act[here, :], dscan[here, :]
        cutd = jnp.where(msk[here, 3:4] > 0.0, step, NEVER)
        fed = step * value
        coefs = pj[here, :]
        one = jnp.zeros((8, chan), F32)
        two = jnp.zeros((8, chan), F32)
        sums = jnp.zeros((8, PAD), F32)
        base = i * 8 * states_n
        for n in range(states_n):
            at = slice(8 * n, 8 * n + 8)
            into = jnp.broadcast_to(coefs[:, ranks + n : ranks + n + 1], (8, chan))
            out = jnp.broadcast_to(coefs[:, ranks + states_n + n : ranks + states_n + n + 1], (8, chan))
            state = h[pl.ds(pl.multiple_of(base + 8 * n, 8), 8), :]
            whole = held[at, :] + out * grads
            passed = jnp.exp2(cutd * rate[at, :]) * whole
            held[at, :] = passed
            moved = passed * before(n)
            sums = jnp.where(lanes == n, jnp.sum(whole * fed, axis=1, keepdims=True), sums)
            sums = jnp.where(lanes == states_n + n, jnp.sum(grads * state, axis=1, keepdims=True), sums)
            one = one + whole * into
            two = two + moved * rate[at, :]
            rsum[at, :] = rsum[at, :] + moved * step
        dbc[here, :] = sums
        dact_o[here, :] = step * one
        draw[here, :] = (value * one + LN2 * two) * (1.0 - jnp.exp(-step))

    def step_fn(back, _):
        i = steps - 1 - back
        base = (i - 1) * 8 * states_n
        one_step(i, lambda n: h[pl.ds(pl.multiple_of(base + 8 * n, 8), 8), :])
        return 0

    lax.fori_loop(0, steps - 1, step_fn, 0)
    one_step(0, lambda n: jnp.where(last, first[8 * n : 8 * n + 8, :], edge[8 * n : 8 * n + 8, :]))
    raws = draw[...]
    pieces = cut(raws)
    dproj_o[0, :ranks, :] = triple(nt, cut(dtw[...]), pieces)
    dproj_o[0, ranks:, :] = dbc[...].T[: 2 * states_n, :]
    dtw_o[...] += triple(nn, cut(proj[0, :ranks, :]), pieces)
    dtb_o[...] += jnp.sum(raws, axis=0, keepdims=True)

    @pl.when(last)
    def _():
        for n in range(states_n):
            at = slice(8 * n, 8 * n + 8)
            dalog_o[n : n + 1, :] = LN2 * jnp.sum(rate[at, :] * rsum[at, :], axis=0, keepdims=True)


def conv_back_kernel(dproj, xp, act, conv, inner, dscan, dact, skip, msk, cw, dinner_o, edge_o, dcw_o, dxp_o, f0, f1, f2):
    rows, chan = act.shape
    fs = (f0, f1, f2)
    xps = cut(xp[...])
    dcw_o[...] = jnp.zeros_like(dcw_o)
    dxp_o[...] = jnp.zeros_like(dxp_o)

    def block_fn(block, _):
        base = pl.multiple_of(block * 128, 128)
        here = pl.ds(base, 128)
        value = act[here, :]
        pieces = cut(dproj[block])
        dxp_o[...] += triple(nn, pieces, cut(value))
        grads = dscan[here, :] * skip[...] + dact[here, :] + triple(tn, pieces, xps)
        summed = conv[here, :]
        soft = sigmoid(summed)
        dconv = grads * (soft * (1.0 + summed * (1.0 - soft)))
        dinner_o[here, :] = dconv * cw[3:4, :]
        dcw_o[4:5, :] += jnp.sum(dconv, axis=0, keepdims=True)
        dcw_o[3:4, :] += jnp.sum(dconv * inner[pl.ds(base + 24, 128), :], axis=0, keepdims=True)
        for k in range(3):
            masked = dconv * msk[here, k : k + 1]
            dcw_o[k : k + 1, :] += jnp.sum(masked * inner[pl.ds(base + 8 * k, 128), :], axis=0, keepdims=True)
            fs[k][here, :] = masked * cw[k : k + 1, :]
        return 0

    lax.fori_loop(0, rows // 128, block_fn, 0)
    edge_o[...] = jnp.zeros_like(edge_o)
    for i in range(3):
        piece = f0[8 * i : 8 * i + 1, :]
        for k in range(1, i + 1):
            piece = piece + fs[k][8 * (i - k) : 8 * (i - k) + 1, :]
        edge_o[i : i + 1, :] = piece
    bottom = lax.broadcasted_iota(jnp.int32, (8, chan), 0) == 7
    for k in range(3):
        for i in range(3 - k):
            turned = pltpu.roll(fs[k][8 * i : 8 * i + 8, :], 7, axis=0)
            fs[k][rows + 8 * i : rows + 8 * i + 8, :] = jnp.where(bottom, 0.0, turned)

    def add_fn(block, _):
        base = pl.multiple_of(block * 128, 128)
        total = dinner_o[pl.ds(base, 128), :]
        for k in range(3):
            total = total + fs[k][pl.ds(base + 8 * (3 - k), 128), :]
        dinner_o[pl.ds(base, 128), :] = total
        return 0

    lax.fori_loop(0, rows // 128, add_fn, 0)


def normed_back_kernel(tail, dinner, after, dgate, w, hid, *refs):
    dn_o, dgain_o, dcat = refs
    chan = dinner.shape[1]
    count = dinner.shape[0]
    dcat[:, :chan] = dinner[...]
    dcat[:, chan:] = dgate[...]
    if tail:
        for i in range(3):
            row = count - 24 + 8 * i + 7
            dcat[row : row + 1, :chan] = dcat[row : row + 1, :chan] + after[i : i + 1, :]
    pieces = cut(dcat[...])
    out = triple(nt, (pieces[0][:, :chan], pieces[1][:, :chan]), cut(w[0]))
    out = out + triple(nt, (pieces[0][:, chan:], pieces[1][:, chan:]), cut(w[1]))
    dn_o[...] = out
    values = hid[...]
    scale = lax.rsqrt(jnp.mean(values * values, axis=1, keepdims=True) + EPS)
    dgain_o[...] = jnp.sum(out * values * scale, axis=0, keepdims=True)


def in_grads_kernel(dinner, after, dgate, hid, gain, dw_o, dcat):
    rows, chan = dinner.shape
    dcat[...] = dinner[...]
    for i in range(3):
        row = rows - 24 + 8 * i + 7
        dcat[row : row + 1, :] = dcat[row : row + 1, :] + after[i : i + 1, :]
    dw_o[...] = jnp.zeros_like(dw_o)

    def block_fn(block, _):
        here = pl.ds(pl.multiple_of(block * 256, 256), 256)
        values = hid[here, :]
        scale = lax.rsqrt(jnp.mean(values * values, axis=1, keepdims=True) + EPS)
        left = cut(values * scale * gain[...])
        dw_o[0] += triple(tn, left, cut(dcat[here, :]))
        dw_o[1] += triple(tn, left, cut(dgate[here, :]))
        return 0

    lax.fori_loop(0, rows // 256, block_fn, 0)


def out_grads_kernel(*refs):
    his, los, dres, out = refs[:QUARTERS], refs[QUARTERS : 2 * QUARTERS], refs[2 * QUARTERS : 3 * QUARTERS], refs[-1]
    for i in range(QUARTERS):
        piece = triple(tn, (his[i][...], los[i][...]), cut(dres[i][...]))
        out[...] = piece if i == 0 else out[...] + piece


def undeal_kernel(pcol, *refs):
    parts, out = refs[:-1], refs[-1]
    count = parts[0].shape[0]
    pieces = [cut3(p[...]) for p in parts]

    def block_fn(block, _):
        here = pl.ds(pl.multiple_of(block * 256, 256), 256)
        total = jnp.zeros((256, out.shape[1]), F32)
        for q, (high, middle, low) in enumerate(pieces):
            marks = col_marks(pcol[here, :], q * count, count)
            total = total + (nn(marks, high) + (nn(marks, middle) + nn(marks, low)))
        out[here, :] = total
        return 0

    lax.fori_loop(0, out.shape[0] // 256, block_fn, 0)


def output_kernel(pcol, *refs):
    rows = refs[:QUARTERS]
    adds = refs[QUARTERS : 2 * QUARTERS]
    out = refs[-1]
    count = rows[0].shape[0]
    pieces = [cut3(r[...] + a[...]) for r, a in zip(rows, adds)]

    def block_fn(block, _):
        here = pl.ds(pl.multiple_of(block * 256, 256), 256)
        total = jnp.zeros((256, out.shape[1]), F32)
        for q, (high, middle, low) in enumerate(pieces):
            marks = col_marks(pcol[here, :], q * count, count)
            total = total + (nn(marks, high) + (nn(marks, middle) + nn(marks, low)))
        out[here, :] = total
        return 0

    lax.fori_loop(0, out.shape[0] // 256, block_fn, 0)


def hidden_grad_kernel(dn0, dn1, dn2, dn3, hid, dres, gain, out):
    for q, dn in enumerate((dn0, dn1, dn2, dn3)):
        count = dn.shape[0]
        here = slice(q * count, (q + 1) * count)
        values = hid[here, :]
        scale = lax.rsqrt(jnp.mean(values * values, axis=1, keepdims=True) + EPS)
        unit = values * scale
        mine = dn[...] * gain[...]
        grad = dres[here, :] + scale * mine - unit * (scale * jnp.mean(mine * unit, axis=1, keepdims=True))
        steps = count // CHUNKS
        out[:, q * steps : (q + 1) * steps, :] = jnp.swapaxes(
            grad.reshape(steps, CHUNKS, grad.shape[1]), 0, 1
        )


def chan_sum(value):
    place = lax.axis_index("chan")
    inward = value + lax.ppermute(value, "chan", [(0, 1), (3, 2)])
    total = inward + lax.ppermute(inward, "chan", [(1, 2), (2, 1)])
    outward = lax.ppermute(total, "chan", [(1, 0), (2, 3)])
    return jnp.where((place == 0) | (place == 3), outward, total)


def small_chan_sum(value):
    count = lax.axis_size("chan")
    got = lax.all_to_all(value, "chan", split_axis=0, concat_axis=0, tiled=True)
    mine = jnp.sum(got.reshape((count, value.shape[0] // count) + value.shape[1:]), axis=0)
    return lax.all_gather(mine, "chan", axis=0, tiled=True)


def exchange(rows, experts):
    blocks = rows.reshape(experts, rows.shape[0] // experts, rows.shape[1])
    got = lax.all_to_all(blocks, "seq", split_axis=0, concat_axis=0, tiled=True)
    return got.reshape(rows.shape)


def body(
    hidden,
    norm1_gain,
    in_weight,
    conv_weight,
    conv_bias,
    xproj_weight,
    dtproj_weight,
    dt_bias,
    a_log,
    skip_weight,
    out_weight,
    norm2_gain,
    router_weight,
    up_weight,
    down_weight,
    seq_lengths,
    expert_ids,
    cotangent,
):
    rows, model = hidden.shape
    chan = conv_weight.shape[1]
    taps = conv_weight.shape[0]
    ranks, states_n = dtproj_weight.shape[0], a_log.shape[0]
    width = ranks + 2 * states_n
    experts = router_weight.shape[1]
    seq_devices = lax.axis_size("seq")
    assert up_weight.shape[0] == 1 and experts == seq_devices and taps == 4
    assert lax.axis_size("chan") == 4 and rows % 1024 == 0
    steps = rows // CHUNKS
    count = rows // QUARTERS
    capacity = max(2, 5 * rows // (4 * experts))
    share = -(-capacity // QUARTERS)
    slots = experts * share
    me = lax.axis_index("seq")
    me_arr = me.astype(jnp.int32).reshape(1)

    def to_major(values):
        return values.reshape(CHUNKS, steps, -1).transpose(1, 0, 2).reshape(rows, -1)

    hid_sm = to_major(hidden)
    rim = lax.ppermute(hidden[rows - 8 :], "seq", [(i, i + 1) for i in range(seq_devices - 1)])
    index = jnp.arange(rows, dtype=jnp.int32)
    places = me * rows + (index % CHUNKS) * steps + index // CHUNKS
    start = jnp.zeros_like(places)
    edge = jnp.zeros((), jnp.int32)
    for i in range(seq_lengths.shape[0] - 1):
        edge = edge + seq_lengths[i]
        start = jnp.where(places >= edge, edge, start)
    offset = places - start
    limits = jnp.array([3, 2, 1, 1, 9, 9, 9, 9], jnp.int32)
    msk = (offset[:, None] >= limits[None, :]).astype(F32)

    chosen = expert_ids[:, 0]
    names = jnp.arange(experts, dtype=jnp.int32)
    onehot = (chosen[:, None] == names[None, :]).astype(BF)
    tri = (index[:, None] >= index[None, :]).astype(BF)
    running = jnp.dot(tri, onehot, preferred_element_type=F32)
    counts = jnp.sum(onehot.astype(F32), axis=0)
    firsts = jnp.sum(jnp.where(names[None, :] < names[:, None], counts[None, :], 0.0), axis=1)
    rank = jnp.sum(onehot.astype(F32) * (running - 1.0 + firsts[None, :]), axis=1).astype(jnp.int32)
    dealt = (rank % QUARTERS) * count + rank // QUARTERS
    dealt_sm = to_major(dealt[:, None])
    firsts_i = firsts.astype(jnp.int32)
    ends_i = firsts_i + counts.astype(jnp.int32)
    quarter = jnp.arange(QUARTERS, dtype=jnp.int32)
    ranks_here = jnp.arange(count, dtype=jnp.int32)[None, :] * QUARTERS + quarter[:, None]
    owner = jnp.sum((ranks_here[:, :, None] >= ends_i[None, None, :]).astype(jnp.int32), axis=2)
    owner_hot = owner[:, :, None] == names[None, None, :]
    lowest = (firsts_i[None, :] - quarter[:, None] + QUARTERS - 1) // QUARTERS
    lowest = jnp.sum(jnp.where(owner_hot, lowest[:, None, :], 0), axis=2)
    slot = owner * share + jnp.arange(count, dtype=jnp.int32)[None, :] - lowest
    owner_f = owner_hot.astype(F32)

    prow = dealt.reshape(1, rows)
    prow_sm = dealt_sm.reshape(1, rows)
    pcol = dealt.reshape(rows, 1)
    gain1, gain2 = norm1_gain.reshape(1, model), norm2_gain.reshape(1, model)
    skip = skip_weight.reshape(1, chan)
    xp = xproj_weight.T
    router_t = router_weight.T

    inner, gate_in, conv, act, proj_part = call(
        enter_kernel,
        (shape((rows + 24, chan)), shape((rows, chan)), shape((rows, chan)), shape((rows, chan)), shape((rows // 128, width, 128))),
        hid_sm, rim, gain1, in_weight, conv_weight, conv_bias.reshape(1, chan), xp, msk,
        scratch=[pltpu.VMEM((model, 2 * chan), BF)] * 2,
        flops=6 * rows * model * 2 * chan,
    )
    hid_p, cot_p = call(
        deal_kernel, (shape((rows, model)), shape((rows, model))), prow, hidden, cotangent,
        flops=12 * rows * rows * model,
    )
    proj = small_chan_sum(proj_part)
    sent_cot = []
    for q in range(QUARTERS):
        part = call(slots_kernel, shape((slots, model)), cot_p[q * count : (q + 1) * count], slot[q : q + 1], flops=6 * slots * count * model)
        sent_cot.append(exchange(part, experts))
    delta, pj, rate, bt, bs, tot = call(
        sweep1_kernel,
        (shape((rows, chan)), shape((rows, PAD)), shape((8 * states_n, chan)), shape((8 * states_n, chan)), shape((8 * states_n, chan)), shape((2 * states_n, chan))),
        proj, dtproj_weight, dt_bias.reshape(1, chan), a_log, act, msk,
        scratch=[pltpu.VMEM((8 * states_n, chan), F32), pltpu.VMEM((rows, chan), F32)],
        flops=20 * rows * chan * states_n,
    )
    gath = lax.all_gather(tot, "seq")
    block_rows = 128
    blocks = rows // block_rows
    grow = (block_rows // 8) * 8 * states_n
    whole = lambda a, b: pl.BlockSpec((a, b), lambda i: (0, 0))
    band = lambda b: pl.BlockSpec((block_rows, b), lambda i: (i, 0))
    small = 8 * states_n
    first, hist, pre, ghi, glo = pl.pallas_call(
        functools.partial(sweep2_kernel, ranks),
        grid=(blocks,),
        in_specs=[
            pl.BlockSpec(memory_space=pltpu.SMEM),
            pl.BlockSpec((seq_devices, 2 * states_n, chan), lambda i: (0, 0, 0)),
            band(chan), band(chan), band(PAD), band(chan), band(8),
            whole(small, chan), whole(small, chan), whole(small, chan), whole(1, chan),
        ],
        out_specs=(
            whole(small, chan),
            pl.BlockSpec((grow, chan), lambda i: (i, 0)),
            band(chan), band(chan), band(chan),
        ),
        out_shape=(
            shape((small, chan)), shape((blocks * grow, chan)), shape((rows, chan)), shape((rows, chan), BF), shape((rows, chan), BF),
        ),
        scratch_shapes=[pltpu.VMEM((small, chan), F32)],
        compiler_params=pltpu.CompilerParams(vmem_limit_bytes=40 << 20),
        cost_estimate=pl.CostEstimate(flops=20 * rows * chan * states_n, bytes_accessed=4 * blocks * grow * chan, transcendentals=rows * chan * states_n),
    )(me_arr, gath, delta, act, pj, gate_in, msk, rate, bt, bs, skip)

    uhi, ulo, dhi, dlo = call(
        weights_kernel, tuple(shape(up_weight.shape[1:], BF) for _ in range(4)), up_weight[0], down_weight[0]
    )
    units = up_weight.shape[2]

    res, gates, softs, his, los, xs, ys, gts, ghs, dn2, dlogs = ([] for _ in range(11))
    for q in range(QUARTERS):
        mixed, hi_q, lo_q = call(
            functools.partial(leave_kernel, q),
            (shape((count, model)), shape((count, chan), BF), shape((count, chan), BF)),
            prow_sm, ghi, glo, out_weight,
            flops=6 * count * chan * model + 4 * count * rows * chan,
        )
        his.append(hi_q)
        los.append(lo_q)
        res_q, slot_q, gate_q, soft_q = call(
            route_kernel,
            (shape((count, model)), shape((slots, model + PAD)), shape((count, 1)), shape((count, experts))),
            chan_sum(mixed), hid_p[q * count : (q + 1) * count], gain2, router_t, owner_f[q], slot[q : q + 1],
            flops=6 * slots * count * model,
        )
        res.append(res_q)
        gates.append(gate_q)
        softs.append(soft_q)
        xs.append(exchange(slot_q, experts))
    for q in range(QUARTERS):
        y_q, dx_q, gt_q, gh_q = call(
            expert_kernel,
            (shape((slots, model)), shape((slots, model + PAD)), shape((slots, units)), shape((slots, units))),
            xs[q], sent_cot[q], uhi, ulo, dhi, dlo,
            flops=24 * slots * model * units,
        )
        ys.append(y_q)
        gts.append(gt_q)
        ghs.append(gh_q)
        part, dlog_q = call(
            home_kernel,
            (shape((count, model)), shape((count, experts))),
            exchange(dx_q, experts), slot[q].reshape(count, 1), gates[q], softs[q], owner_f[q], router_t,
            flops=6 * slots * count * model,
        )
        dlogs.append(dlog_q)
        dn2.append(chan_sum(part))
    dres, dgps, dgain2s, drouters = [], [], [], []
    for q in range(QUARTERS):
        dres_q, dgp_q, dgain_q, drouter_q = call(
            resid_kernel,
            (shape((count, model)), shape((count, chan)), shape((1, model)), shape((experts, model))),
            dn2[q], res[q], cot_p[q * count : (q + 1) * count], gain2, out_weight, dlogs[q],
            flops=6 * count * chan * model,
        )
        dres.append(dres_q)
        dgps.append(dgp_q)
        dgain2s.append(dgain_q)
        drouters.append(drouter_q)

    dscan, dgate, dskip, rbt, rbs, rtot = call(
        functools.partial(back1_kernel, ranks),
        (shape((rows, chan)), shape((rows, chan)), shape((1, chan)), shape((small, chan)), shape((small, chan)), shape((2 * states_n, chan))),
        *dgps, dealt_sm, gate_in, pre, act, delta, msk, pj, rate,
        scratch=[pltpu.VMEM((small, chan), F32), pltpu.VMEM((rows, chan), F32)],
        flops=20 * rows * chan * states_n,
    )
    rgath = lax.all_gather(rtot, "seq")

    backs = []
    for q in range(QUARTERS):
        got = exchange(ys[q], experts)
        part = call(
            home_out_kernel, shape((count, model)), got, slot[q].reshape(count, 1), gates[q],
            flops=6 * slots * count * model,
        )
        backs.append(chan_sum(part))
    output = call(output_kernel, shape((rows, model)), pcol, *res, *backs, flops=6 * rows * rows * model)

    dup, ddown = call(
        expert_grads_kernel, (shape((model, units)), shape((units, model))), *xs, *sent_cot, *gts, *ghs,
        flops=12 * QUARTERS * slots * model * units,
    )
    d_outw = call(out_grads_kernel, shape((chan, model)), *his, *los, *dres, flops=6 * rows * chan * model)
    dres_sm = call(undeal_kernel, shape((rows, model)), dealt_sm, *dres, flops=6 * rows * rows * model)

    rband = lambda b: pl.BlockSpec((block_rows, b), lambda i: (blocks - 1 - i, 0))
    per = grow // small
    dact, dproj_part, d_dtw, d_dtb, d_alog = pl.pallas_call(
        functools.partial(back2_kernel, ranks),
        grid=(blocks,),
        in_specs=[
            pl.BlockSpec(memory_space=pltpu.SMEM),
            pl.BlockSpec((seq_devices, 2 * states_n, chan), lambda i: (0, 0, 0)),
            whole(small, chan),
            rband(chan), rband(chan), rband(PAD),
            pl.BlockSpec((1, width, block_rows), lambda i: (blocks - 1 - i, 0, 0)),
            rband(chan), rband(8),
            pl.BlockSpec((grow, chan), lambda i: (blocks - 1 - i, 0)),
            pl.BlockSpec((small, chan), lambda i: (jnp.maximum((blocks - 1 - i) * per - 1, 0), 0)),
            whole(small, chan), whole(small, chan), whole(small, chan), whole(ranks, chan),
        ],
        out_specs=(
            rband(chan),
            pl.BlockSpec((1, width, block_rows), lambda i: (blocks - 1 - i, 0, 0)),
            whole(ranks, chan), whole(1, chan), whole(states_n, chan),
        ),
        out_shape=(
            shape((rows, chan)), shape((blocks, width, block_rows)), shape((ranks, chan)), shape((1, chan)), shape((states_n, chan)),
        ),
        scratch_shapes=[
            pltpu.VMEM((small, chan), F32), pltpu.VMEM((small, chan), F32), pltpu.VMEM((block_rows, chan), F32), pltpu.VMEM((block_rows, PAD), F32),
        ],
        compiler_params=pltpu.CompilerParams(vmem_limit_bytes=40 << 20),
        cost_estimate=pl.CostEstimate(flops=40 * rows * chan * states_n, bytes_accessed=4 * blocks * grow * chan, transcendentals=rows * chan * states_n),
    )(me_arr, rgath, first, delta, act, pj, proj, dscan, msk, hist, hist, rate, rbt, rbs, dtproj_weight)
    dproj = small_chan_sum(dproj_part)
    dinner, edge_rows, d_conv, d_xp = call(
        conv_back_kernel,
        (shape((rows, chan)), shape((8, chan)), shape((8, chan)), shape((width, chan))),
        dproj, xp, act, conv, inner, dscan, dact, skip, msk, conv_weight,
        scratch=[pltpu.VMEM((rows + 24, chan), F32)] * 3,
        flops=12 * rows * width * chan,
    )
    after = lax.ppermute(edge_rows, "seq", [(i + 1, i) for i in range(seq_devices - 1)])
    dns, dgain1s = [], []
    for q in range(QUARTERS):
        here = slice(q * count, (q + 1) * count)
        dn_q, dgain_q = call(
            functools.partial(normed_back_kernel, q == QUARTERS - 1),
            (shape((count, model)), shape((1, model))),
            dinner[here], after, dgate[here], in_weight, hid_sm[here],
            scratch=[pltpu.VMEM((count, 2 * chan), F32)],
            flops=6 * count * model * 2 * chan,
        )
        dgain1s.append(dgain_q)
        dns.append(chan_sum(dn_q))
    d_inw = call(
        in_grads_kernel, shape((2, model, chan)), dinner, after, dgate, hid_sm, gain1,
        scratch=[pltpu.VMEM((rows, chan), F32)],
        flops=6 * rows * model * 2 * chan,
    )
    hidden_grad = call(
        hidden_grad_kernel, shape((CHUNKS, steps, model)), *dns, hid_sm, dres_sm, gain1,
    ).reshape(rows, model)

    d_gain1, d_router = lax.psum((sum(dgain1s)[0], sum(drouters)), ("seq", "chan"))
    sums = lax.psum(
        (d_inw, d_conv[:4], d_conv[4], d_xp, d_dtw, d_dtb[0], d_alog, dskip[0], d_outw, sum(dgain2s)[0]),
        "seq",
    )
    return (
        output,
        hidden_grad,
        d_gain1,
        sums[0],
        sums[1],
        sums[2],
        sums[3].T,
        sums[4],
        sums[5],
        sums[6],
        sums[7],
        sums[8],
        sums[9],
        d_router.T,
        dup[None],
        ddown[None],
    )


def solution(mesh):
    placed = (
        P("seq", None),
        P(),
        P(None, None, "chan"),
        P(None, "chan"),
        P("chan"),
        P("chan", None),
        P(None, "chan"),
        P("chan"),
        P(None, "chan"),
        P("chan"),
        P("chan", None),
        P(),
        P(),
        P("seq", None, "chan"),
        P("seq", "chan", None),
        P(),
        P("seq", None),
        P("seq", None),
    )
    return jax.shard_map(
        body,
        mesh=mesh,
        in_specs=placed,
        out_specs=(
            P("seq", None),
            P("seq", None),
            P(),
            P(None, None, "chan"),
            P(None, "chan"),
            P("chan"),
            P("chan", None),
            P(None, "chan"),
            P("chan"),
            P(None, "chan"),
            P("chan"),
            P("chan", None),
            P(),
            P(),
            P("seq", None, "chan"),
            P("seq", "chan", None),
        ),
        check_vma=False,
    )
```
